32 devices in a mesh: rep: 8 (over y, x, core), shard: 4 (over z).
Axes of the slice: x: 2, y: 2, z: 4, core: 2. Of those that a mesh axis runs over, the one named last changes fastest.
Arguments:
- features: bfloat16 [32, 28, 28, 704], P(('rep', 'shard')), may hold values from -6 to 6
- cotangent: bfloat16 [32, 28, 28, 704], P(('rep', 'shard')), may hold values from -6 to 6
- dw_kernel: float32 [49, 704], replicated, may hold values from -0.875 to 0.875
- norm_gain: float32 [704], replicated, may hold values from 0.1 to 1.9
- w_expand: bfloat16 [2816, 704], P('shard'), may hold values from -1 to 1
- grn_gamma: float32 [2816], replicated, may hold values from -3 to 3
- grn_beta: float32 [2816], replicated, may hold values from -3 to 3
- w_reduce: bfloat16 [2816, 704], P('shard'), may hold values from -0.109375 to 0.109375
Outputs:
- block_out: bfloat16 [32, 28, 28, 704], P(('rep', 'shard'))
- grad_features: bfloat16 [32, 28, 28, 704], P(('rep', 'shard'))
- grad_kernel: float32 [49, 704], replicated
- grad_gain: float32 [704], replicated
- grad_expand: float32 [2816, 704], P('shard')
- grad_gamma: float32 [2816], replicated
- grad_beta: float32 [2816], replicated
- grad_reduce: float32 [2816, 704], P('shard')
The draws below stay inside these ranges and needn't reach their ends.
All inputs are finite; a program needn't handle non-finite values.
Results may differ from the reference program's by a relative error of at most 0.02.
Values may be sent and summed in bfloat16 or wider, within the bound.
A program may use at most 320 MiB of HBM per device.

```python
import math
import jax
import jax.numpy as jnp
from jax import lax

C = 704
H = 2816
SIDE = 28
IMG_DEV = 1
IMAGES = 32
N_REP = 8
N_SHARD = 4


def draw_w_expand(key, part):
    first_key, second_key = jax.random.split(jax.random.fold_in(key, 11))
    row_scale = jnp.exp(jax.random.uniform(second_key, (H, 1), jnp.float32, math.log(0.3), math.log(3.0)))
    base = jax.random.normal(first_key, (H, C), jnp.float32)
    scaled = jnp.clip(base * row_scale * C ** (-0.5), -1.0, 1.0)
    return scaled.astype(jnp.bfloat16)


def block_levels(key, dims, cuts, low, high):
    def one(axis_at, shards_of):
        heights = jax.random.uniform(jax.random.fold_in(jax.random.fold_in(key, 6), axis_at), (shards_of,), jnp.float32, low / len(cuts), high / len(cuts))
        return jnp.repeat(jnp.exp(heights), dims[axis_at] // shards_of).reshape((-1,) + (1,) * (len(dims) - axis_at - 1))

    gain = one(*cuts[0])
    for cut in cuts[1:]:
        gain = gain * one(*cut)
    return gain


def normal_values(own_key, dims, scale, limit, cuts=(), held_as=jnp.bfloat16):
    entries = scale * jax.random.normal(own_key, dims, jnp.float32)
    if cuts:
        entries = entries * block_levels(own_key, dims, cuts, -0.22, 0.18)
    return jnp.clip(entries, -limit, limit).astype(held_as)


def setup_inputs(seed: int = 0) -> dict:
    key_list = jax.random.split(jax.random.key(seed), 9)
    features = normal_values(key_list[0], (IMAGES, SIDE, SIDE, C), 1.0, 6.0, ((0, 32),))
    cotangent = normal_values(key_list[1], (IMAGES, SIDE, SIDE, C), 1.0, 6.0, ((0, 32),))
    dw_kernel = normal_values(key_list[2], (49, C), 49 ** -0.5, 0.875, (), jnp.float32)
    norm_gain = jnp.clip(1.0 + 0.18 * jax.random.normal(key_list[3], (C,), jnp.float32), 0.1, 1.9)
    w_expand = draw_w_expand(jax.random.fold_in(key_list[8], 71), 0)
    grn_gamma = normal_values(key_list[5], (H,), 0.5, 3.0, (), jnp.float32)
    grn_beta = normal_values(key_list[6], (H,), 0.5, 3.0, (), jnp.float32)
    w_reduce = normal_values(key_list[7], (H, C), H ** -0.5, 0.109375, ((0, 4),))
    return dict(features=features, cotangent=cotangent, dw_kernel=dw_kernel, norm_gain=norm_gain, w_expand=w_expand, grn_gamma=grn_gamma, grn_beta=grn_beta, w_reduce=w_reduce)


def stem_norm(images, dw_kernel, norm_gain):
    height = images.shape[1]
    breadth = images.shape[2]
    padded = jnp.pad(images, ((0, 0), (3, 3), (3, 3), (0, 0)))
    filtered = jnp.zeros_like(images)
    for offset_row in range(7):
        for offset_col in range(7):
            filtered = filtered + dw_kernel[offset_row * 7 + offset_col] * padded[:, offset_row:offset_row + height, offset_col:offset_col + breadth, :]
    centre = lax.optimization_barrier(jnp.mean(filtered, axis=-1, keepdims=True))
    shifted = filtered - centre
    spread = lax.optimization_barrier(jnp.mean(shifted * shifted, axis=-1, keepdims=True))
    return shifted * lax.rsqrt(spread + 1e-06) * norm_gain

def hidden_map(preact, grn_gamma, grn_beta):
    active = jax.nn.gelu(preact, approximate=False)
    energy = jnp.sqrt(lax.optimization_barrier(jnp.sum(active * active, axis=(1, 2), keepdims=True)) + 1e-06)
    ratio_map = energy / (lax.optimization_barrier(jnp.mean(energy, axis=-1, keepdims=True)) + 1e-06)
    return grn_gamma * (active * ratio_map) + grn_beta + active

def contract_rows(left_cols, right_cols):
    return lax.dot_general(left_cols, right_cols, (((0,), (0,)), ((), ())), preferred_element_type=jnp.float32)

def device_pass(features, cotangent, dw_kernel, norm_gain, w_expand, grn_gamma, grn_beta, w_reduce):
    images = features.astype(jnp.float32)
    normed, stem_back = jax.vjp(stem_norm, images, dw_kernel, norm_gain)
    normed_b = normed.astype(jnp.bfloat16)
    tokens = images.shape[0] * images.shape[1] * images.shape[2]
    rows_in = normed_b.reshape(tokens, -1)
    preact = lax.dot_general(rows_in, w_expand, (((1,), (1,)), ((), ())), preferred_element_type=jnp.float32)
    hidden_shape = images.shape[:3] + (w_expand.shape[0],)
    mapped, map_back = jax.vjp(hidden_map, preact.reshape(hidden_shape), grn_gamma, grn_beta)
    mapped_b = mapped.astype(jnp.bfloat16).reshape(tokens, -1)
    branch = jnp.dot(mapped_b, w_reduce, preferred_element_type=jnp.float32)
    block_out = (images + branch.reshape(images.shape)).astype(jnp.bfloat16)
    upstream = cotangent.reshape(tokens, -1)
    back_mapped = lax.dot_general(upstream, w_reduce, (((1,), (1,)), ((), ())), preferred_element_type=jnp.float32)
    back_preact, back_gamma, back_beta = map_back(back_mapped.reshape(hidden_shape))
    back_preact_b = back_preact.astype(jnp.bfloat16).reshape(tokens, -1)
    back_normed = jnp.dot(back_preact_b, w_expand, preferred_element_type=jnp.float32)
    back_images, back_kernel, back_gain = stem_back(back_normed.reshape(images.shape))
    grad_features = (cotangent.astype(jnp.float32) + back_images).astype(jnp.bfloat16)
    term_block = jnp.concatenate([contract_rows(back_preact_b, rows_in), contract_rows(mapped_b, upstream)], axis=1)
    term_block = lax.optimization_barrier(term_block.astype(jnp.bfloat16)).astype(jnp.float32)
    return (block_out, grad_features, term_block, back_kernel, back_gain, back_gamma, back_beta)

def reference(features, cotangent, dw_kernel, norm_gain, w_expand, grn_gamma, grn_beta, w_reduce):
    devices = N_REP * N_SHARD
    stacked_shape = (devices, IMG_DEV) + features.shape[1:]
    stacked = (features.reshape(stacked_shape), cotangent.reshape(stacked_shape))

    def one_device(carry, pair):
        results = device_pass(pair[0], pair[1], dw_kernel, norm_gain, w_expand, grn_gamma, grn_beta, w_reduce)
        updated = tuple((carry[slot] + results[slot + 2] for slot in range(5)))
        return (updated, (results[0], results[1]))
    initial = (jnp.zeros((H, 2 * C), jnp.float32), jnp.zeros((49, C), jnp.float32), jnp.zeros((C,), jnp.float32), jnp.zeros((H,), jnp.float32), jnp.zeros((H,), jnp.float32))
    sums, (outputs, grads) = lax.scan(one_device, initial, stacked)
    inverse = 1.0 / IMAGES
    block_out = outputs.reshape(features.shape)
    grad_features = grads.reshape(features.shape)
    grad_expand = sums[0][:, :C] * inverse
    grad_reduce = sums[0][:, C:] * inverse
    return (block_out, grad_features, sums[1] * inverse, sums[2] * inverse, grad_expand, sums[3] * inverse, sums[4] * inverse, grad_reduce)
```

```python
import jax
import jax.numpy as jnp
from jax import lax
from jax.experimental import pallas as pl
from jax.experimental.pallas import tpu as pltpu
from jax.sharding import Mesh
from jax.sharding import PartitionSpec as P

LANES = 128
VMEM_BYTES = 60 * 1024 * 1024


def up(value, step):
    return -(-value // step) * step


def spread_shifts(shifts, pad, row, value, reach, flip):
    breadth, channels = value.shape
    for b in range(2 * reach + 1):
        move = (reach - b) if flip else (b - reach)
        dst, src = max(0, -move), max(0, move)
        count = breadth - abs(move)
        shifts[b, row + pad, dst : dst + count, :channels] = value[src : src + count]


def stem_kernel(x_ref, k_ref, gain_ref, filtered_ref, normed_ref, shifts, filt):
    height, breadth, channels = x_ref.shape
    wide = shifts.shape[3]
    taps = 7
    reach = 3
    block = 4 if height % 4 == 0 else 1
    shifts[...] = jnp.zeros_like(shifts)

    @pl.loop(0, height)
    def _(row):
        spread_shifts(shifts, reach, row, x_ref[row].astype(jnp.float32), reach, False)

    @pl.loop(0, height // block)
    def _(step):
        base = step * block

        @pl.loop(0, wide // LANES)
        def _(chunk):
            lanes = pl.ds(pl.multiple_of(chunk * LANES, LANES), LANES)
            total = [jnp.zeros((shifts.shape[2], LANES), jnp.float32) for _ in range(block)]
            for b in range(taps):
                weights = [k_ref[pl.ds(a * taps + b, 1), lanes] for a in range(taps)]
                for r in range(block + taps - 1):
                    x = shifts[b, base + r, :, lanes]
                    for a in range(taps):
                        if 0 <= r - a < block:
                            total[r - a] = total[r - a] + weights[a] * x
            for r in range(block):
                filt[base + r, :, lanes] = total[r]

    gain = gain_ref[...]

    @pl.loop(0, height)
    def _(row):
        filtered = filt[row, :breadth, :channels]
        shifted = filtered - jnp.mean(filtered, axis=-1, keepdims=True)
        spread = jnp.mean(shifted * shifted, axis=-1, keepdims=True)
        filtered_ref[row] = filtered
        normed_ref[row] = (shifted * lax.rsqrt(spread + 1e-06) * gain).astype(jnp.bfloat16)


def stem_back_kernel(
    g_ref, filtered_ref, x_ref, cot_ref, k_ref, gain_ref,
    grad_ref, dk_ref, dgain_ref, shifts, image, dimage, partial,
):
    height, breadth, channels = x_ref.shape
    wide = shifts.shape[3]
    deep = shifts.shape[2]
    taps = 7
    reach = 3
    block = 4 if height % 4 == 0 else 1
    shifts[...] = jnp.zeros_like(shifts)
    image[...] = jnp.zeros_like(image)
    partial[...] = jnp.zeros_like(partial)
    dgain_ref[...] = jnp.zeros_like(dgain_ref)
    gain = gain_ref[...]

    @pl.loop(0, height)
    def _(row):
        filtered = filtered_ref[row]
        shifted = filtered - jnp.mean(filtered, axis=-1, keepdims=True)
        inv = lax.rsqrt(jnp.mean(shifted * shifted, axis=-1, keepdims=True) + 1e-06)
        unit = shifted * inv
        back = g_ref[row]
        dgain_ref[...] += jnp.sum(back * unit, axis=0, keepdims=True)
        back = back * gain
        along = jnp.mean(back * unit, axis=-1, keepdims=True)
        dfilt = inv * (back - jnp.mean(back, axis=-1, keepdims=True) - unit * along)
        spread_shifts(shifts, reach, row, dfilt, reach, True)
        image[row, :breadth, :channels] = x_ref[row].astype(jnp.float32)

    @pl.loop(0, height // block)
    def _(step):
        base = step * block

        @pl.loop(0, wide // LANES)
        def _(chunk):
            lanes = pl.ds(pl.multiple_of(chunk * LANES, LANES), LANES)
            images = [image[base + r, :, lanes] for r in range(block)]
            total = [jnp.zeros((deep, LANES), jnp.float32) for _ in range(block)]
            for b in range(taps):
                weights = [k_ref[pl.ds(a * taps + b, 1), lanes] for a in range(taps)]
                sums = [jnp.zeros((8, LANES), jnp.float32) for _ in range(taps)]
                for r in range(block + taps - 1):
                    d = shifts[b, base + r, :, lanes]
                    for a in range(taps):
                        p = r - (taps - 1) + a
                        if 0 <= p < block:
                            total[p] = total[p] + weights[a] * d
                            product = images[p] * d
                            for q in range(0, deep, 8):
                                sums[a] = sums[a] + product[q : q + 8]
                for a in range(taps):
                    partial[a * taps + b, :, lanes] += sums[a]
            for r in range(block):
                dimage[base + r, :, lanes] = total[r]

    @pl.loop(0, height)
    def _(row):
        grad_ref[row] = (
            cot_ref[row].astype(jnp.float32) + dimage[row, :breadth, :channels]
        ).astype(jnp.bfloat16)

    dk_ref[...] = jnp.sum(partial[...], axis=1)[:, :channels]


def stem_forward(x, taps, gain):
    height, breadth, channels = x.shape
    deep, wide = up(breadth, 8), up(channels, LANES)
    whole = pl.BlockSpec(memory_space=pltpu.VMEM)
    return pl.pallas_call(
        stem_kernel,
        out_shape=(
            jax.ShapeDtypeStruct(x.shape, jnp.float32),
            jax.ShapeDtypeStruct(x.shape, jnp.bfloat16),
        ),
        in_specs=[whole] * 3,
        out_specs=(whole,) * 2,
        scratch_shapes=[
            pltpu.VMEM((7, height + 6, deep, wide), jnp.float32),
            pltpu.VMEM((height, deep, wide), jnp.float32),
        ],
        cost_estimate=pl.CostEstimate(
            flops=98 * x.size, bytes_accessed=8 * x.size, transcendentals=0
        ),
        compiler_params=pltpu.CompilerParams(vmem_limit_bytes=VMEM_BYTES),
        name="stem_forward",
    )(x, taps, gain)


def stem_backward(back, filtered, x, cot, taps, gain):
    height, breadth, channels = x.shape
    deep, wide = up(breadth, 8), up(channels, LANES)
    whole = pl.BlockSpec(memory_space=pltpu.VMEM)
    return pl.pallas_call(
        stem_back_kernel,
        out_shape=(
            jax.ShapeDtypeStruct(x.shape, jnp.bfloat16),
            jax.ShapeDtypeStruct((49, channels), jnp.float32),
            jax.ShapeDtypeStruct((1, channels), jnp.float32),
        ),
        in_specs=[whole] * 6,
        out_specs=(whole,) * 3,
        scratch_shapes=[
            pltpu.VMEM((7, height + 6, deep, wide), jnp.float32),
            pltpu.VMEM((height, deep, wide), jnp.float32),
            pltpu.VMEM((height, deep, wide), jnp.float32),
            pltpu.VMEM((49, 8, wide), jnp.float32),
        ],
        cost_estimate=pl.CostEstimate(
            flops=196 * x.size, bytes_accessed=16 * x.size, transcendentals=0
        ),
        compiler_params=pltpu.CompilerParams(vmem_limit_bytes=VMEM_BYTES),
        name="stem_backward",
    )(back, filtered, x, cot, taps, gain)


def hidden_map(preacts, gammas, betas):
    actives = [jax.nn.gelu(preact, approximate=False) for preact in preacts]
    energies = [
        jnp.sqrt(jnp.sum(active * active, axis=1, keepdims=True) + 1e-06) for active in actives
    ]
    units = sum(energy.shape[-1] for energy in energies)
    mean = sum(jnp.sum(energy, axis=-1, keepdims=True) for energy in energies) / units
    return [
        gamma * (active * (energy / (mean + 1e-06))) + beta + active
        for active, energy, gamma, beta in zip(actives, energies, gammas, betas)
    ]


def contract_rows(left_cols, right_cols):
    return lax.dot_general(
        left_cols, right_cols, (((0,), (0,)), ((), ())), preferred_element_type=jnp.float32
    )


def against_rows(left_cols, pieces):
    return lax.dot_general(
        left_cols, pieces, (((1,), (1,)), ((), ())), preferred_element_type=jnp.float32
    )


def shards(features, cotangent, dw_kernel, norm_gain, w_expand, grn_gamma, grn_beta, w_reduce):
    pair = lax.axis_size("core")
    shard_count = lax.axis_size("shard")
    core = lax.axis_index("core")
    count = features.shape[0]
    local, channels = w_expand.shape
    half = local // pair
    swap_pairs = [(i, pair - 1 - i) for i in range(pair)]

    def exchange(value):
        return lax.ppermute(value, "core", swap_pairs)

    def gathered(weight):
        mine = lax.dynamic_slice_in_dim(weight, core * half, half, axis=0)
        rows = lax.all_gather(mine, "shard", axis=0, tiled=True)
        return [rows, exchange(rows)]

    def mine_first(vector):
        split = vector.reshape(shard_count, pair, half)
        flipped = split[:, ::-1]
        ordered = jnp.where(core == 0, split, flipped)
        return [ordered[:, i].reshape(shard_count * half) for i in range(pair)]

    def in_order(parts):
        ordered = jnp.stack([part.reshape(shard_count, half) for part in parts], axis=1)
        return jnp.where(core == 0, ordered, ordered[:, ::-1]).reshape(-1)

    expand = gathered(w_expand)
    reduce = gathered(w_reduce)

    taps = jnp.pad(dw_kernel, ((0, 0), (0, up(channels, LANES) - channels)))
    gain = norm_gain.reshape(1, channels)
    stems = [stem_forward(features[i], taps, gain) for i in range(count)]
    positions = features.shape[1] * features.shape[2]
    tokens = count * positions
    rows_in = jnp.stack([stem[1] for stem in stems]).reshape(tokens, channels)
    upstream = cotangent.reshape(tokens, channels)

    preacts = [against_rows(rows_in, w).reshape(count, positions, -1) for w in expand]
    mapped, map_back = jax.vjp(hidden_map, preacts, mine_first(grn_gamma), mine_first(grn_beta))
    mapped = [m.astype(jnp.bfloat16).reshape(tokens, -1) for m in mapped]

    def reduced_term(terms):
        other = exchange(terms[1].astype(jnp.bfloat16))
        both = terms[0].astype(jnp.bfloat16).astype(jnp.float32) + other.astype(jnp.float32)
        rows = lax.psum_scatter(
            both.astype(jnp.bfloat16), "shard", scatter_dimension=0, tiled=True
        )
        return lax.psum(rows, "rep")

    sum_reduce = reduced_term([contract_rows(m, upstream) for m in mapped])
    back_mapped = [against_rows(upstream, w).reshape(count, positions, -1) for w in reduce]
    back_preact, back_gamma, back_beta = map_back(back_mapped)
    back_preact = [b.astype(jnp.bfloat16).reshape(tokens, -1) for b in back_preact]
    sum_expand = reduced_term([contract_rows(b, rows_in) for b in back_preact])

    branch = sum(
        jnp.dot(m, w, preferred_element_type=jnp.float32) for m, w in zip(mapped, reduce)
    )
    block_out = (features.astype(jnp.float32) + branch.reshape(features.shape)).astype(
        jnp.bfloat16
    )
    back_normed = sum(
        jnp.dot(b, w, preferred_element_type=jnp.float32) for b, w in zip(back_preact, expand)
    ).reshape(features.shape)
    backs = [
        stem_backward(back_normed[i], stems[i][0], features[i], cotangent[i], taps, gain)
        for i in range(count)
    ]
    grad_features = jnp.stack([back[0] for back in backs])
    small = jnp.concatenate(
        [
            sum(back[1] for back in backs).reshape(-1),
            sum(back[2] for back in backs).reshape(-1),
            in_order(back_gamma),
            in_order(back_beta),
        ]
    )
    small = lax.psum(small, ("rep", "core", "shard"))
    inverse = 1.0 / (count * lax.axis_size("rep") * pair * shard_count)
    small = small * inverse
    ends = [dw_kernel.size, dw_kernel.size + channels]
    ends.append(ends[1] + grn_gamma.size)

    def whole_rows(rows):
        other = exchange(rows)
        first = jnp.where(core == 0, rows, other)
        second = jnp.where(core == 0, other, rows)
        return jnp.concatenate([first, second]).astype(jnp.float32) * inverse

    return (
        block_out,
        grad_features,
        small[: ends[0]].reshape(dw_kernel.shape),
        small[ends[0] : ends[1]],
        whole_rows(sum_expand),
        small[ends[1] : ends[2]],
        small[ends[2] :],
        whole_rows(sum_reduce),
    )


def solution(mesh):
    rep, shard = mesh.shape["rep"], mesh.shape["shard"]
    split = Mesh(mesh.devices.reshape(rep // 2, 2, shard), ("rep", "core", "shard"))
    maps = P(("rep", "core", "shard"), None, None, None)
    return jax.shard_map(
        shards,
        mesh=split,
        in_specs=(maps, maps, P(), P(), P("shard", None), P(), P(), P("shard", None)),
        out_specs=(maps, maps, P(), P(), P("shard", None), P(), P(), P("shard", None)),
        check_vma=False,
    )
```
